128 devices in a mesh: dp: 16 (over z_lo, x, core), mp: 8 (over z_hi, y).
Axes of the slice: x: 4, y: 4, z: 4 (z_hi: 2, z_lo: 2; z = z_hi * 2 + z_lo), core: 2. Of those that a mesh axis runs over, the one named last changes fastest.
Arguments:
- acts: bfloat16 [8192, 3072], P('dp'), may hold values from -16 to 16
- grads_out: bfloat16 [8192, 16384], P('dp', 'mp'), may hold values from -0.088388348 to 0.088388348
- old_a: float32 [16, 3, 64, 1024], P('dp'), may hold values from -0.0625 to 0.0625
- old_g: float32 [8, 16, 2, 64, 1024], P('mp', 'dp'), may hold values from -0.0625 to 0.0625
- a_inverse: bfloat16 [3072, 1024], P('dp'), may hold values from -0.1875 to 0.1875
- g_inverse: bfloat16 [16384, 1024], P('mp'), may hold values from -0.1875 to 0.1875
- owner_map: int32 [5, 16], replicated, may hold values from 0 to 15, each once within a row
Outputs:
- a_factor: float32 [16, 3, 64, 1024], P('dp')
- g_factor: float32 [8, 16, 2, 64, 1024], P('mp', 'dp')
- preconditioned: bfloat16 [3072, 8, 2048], P(None, 'mp', 'dp')
The draws below stay inside these ranges and needn't reach their ends.
Inputs may be any that keep to these rules, and one draw needn't show every extreme that they name: `owner_map`: each row is a permutation: row k tells, for each of the 16 row strips of factor block k, which dp index holds it. Rows 0 to 2 are the activation blocks, the others the output-gradient blocks of every mp index.
All inputs are finite; a program needn't handle non-finite values.
Results may differ from the reference program's by a relative error of at most 0.02.
Values may be sent and summed in bfloat16 or wider, within the bound.
No kernel may reach another device: no remote copies, remote signals or barrier semaphores. Data moves between devices by JAX's collectives and lax.ppermute only.
A program may use at most 128 MiB of HBM per device.

```python
import jax
import jax.numpy as jnp
from jax import lax

D_WIN = 3072
BLOCK = 1024
FF_DEV = 2048
TOK_DEV = 512
TOKENS = 8192
FF_WIN = 16384
NA = 3
NG = 2
STRIP = 64
N_DP = 16
N_MP = 8


def draw_acts(key, part):
    values = jnp.clip(jax.random.normal(jax.random.fold_in(key, 23), (TOKENS, D_WIN), jnp.float32), -5.0, 5.0)
    pairing = jax.random.permutation(jax.random.fold_in(key, 29), N_DP)
    token_block = jnp.arange(TOKENS, dtype=jnp.int32) // TOK_DEV
    feature_block = jnp.arange(D_WIN, dtype=jnp.int32) // (D_WIN // N_DP)
    paired = pairing[token_block][:, None] == feature_block[None, :]
    return jnp.where(paired, 3.0 * values, values).astype(jnp.bfloat16)


def draw_grads_out(key, part):
    spread = TOKENS ** (-0.5)
    values = jnp.clip(jax.random.normal(jax.random.fold_in(key, 37), (TOKENS, FF_WIN), jnp.float32), -6.0, 6.0)
    return (values * spread).astype(jnp.bfloat16)


def levels(own_key, shape, shards, smallest, top_value):
    def one(position, shards_of):
        steps = jax.random.uniform(jax.random.fold_in(jax.random.fold_in(own_key, 6), position), (shards_of,), jnp.float32, smallest / len(shards), top_value / len(shards))
        return jnp.repeat(jnp.exp(steps), shape[position] // shards_of).reshape((-1,) + (1,) * (len(shape) - position - 1))

    loudness = one(*shards[0])
    for cut in shards[1:]:
        loudness = loudness * one(*cut)
    return loudness


def normal_values(key, extent, scale, limit, shards=(), held_as=jnp.bfloat16):
    entries = jax.random.normal(key, extent, jnp.float32) * scale
    if len(shards) > 0:
        entries = levels(key, extent, shards, -0.22, 0.18) * entries
    return jnp.clip(entries, min=-limit, max=limit).astype(held_as)


def setup_inputs(seed: int = 0) -> dict:
    arg_keys = jax.random.split(jax.random.key(seed), 8)
    acts = draw_acts(jax.random.fold_in(arg_keys[7], 71), 0)
    grads_out = draw_grads_out(jax.random.fold_in(arg_keys[7], 71), 0)
    old_a = normal_values(arg_keys[2], (N_DP, NA, STRIP, BLOCK), (TOKENS ** -0.5), 0.0625, ((0, 16),), jnp.float32)
    old_g = normal_values(arg_keys[3], (N_MP, N_DP, NG, STRIP, BLOCK), (TOKENS ** -0.5), 0.0625, ((0, 8), (1, 16)), jnp.float32)
    a_inverse = normal_values(arg_keys[4], (D_WIN, BLOCK), BLOCK ** -0.5, 0.1875, ((0, 16),))
    g_inverse = normal_values(arg_keys[5], (FF_WIN, BLOCK), BLOCK ** -0.5, 0.1875, ((0, 8),))
    owner_map = jax.vmap(lambda own: jax.random.permutation(own, N_DP))(jax.random.split(arg_keys[6], (NA + NG))).reshape((NA + NG, N_DP)).astype(jnp.int32)
    return {"acts": acts, "grads_out": grads_out, "old_a": old_a, "old_g": old_g, "a_inverse": a_inverse, "g_inverse": g_inverse, "owner_map": owner_map}


decay_rate = 0.75


def accumulate(running, pieces):
    act_rows, grad_rows = pieces
    act_blocks = act_rows.reshape(TOK_DEV, NA, BLOCK).astype(jnp.float32)
    grad_blocks = grad_rows.reshape(TOK_DEV, N_MP * NG, BLOCK).astype(jnp.float32)
    act_cov = jnp.einsum('tkb,tkc->kbc', act_blocks, act_blocks) / (TOK_DEV * N_DP)
    grad_cov = jnp.einsum('tkb,tkc->kbc', grad_blocks, grad_blocks)
    partial_grad = jnp.dot(act_rows.T, grad_rows, preferred_element_type=jnp.float32).astype(jnp.bfloat16)
    partial_grad = lax.optimization_barrier(partial_grad).astype(jnp.float32)
    return (running[0] + act_cov, running[1] + grad_cov, running[2] + partial_grad), None


def reference(acts, grads_out, old_a, old_g, a_inverse, g_inverse, owner_map):
    acts_split = acts.reshape(N_DP, TOK_DEV, D_WIN)
    grads_split = grads_out.reshape(N_DP, TOK_DEV, FF_WIN)
    start_state = (jnp.zeros((NA, BLOCK, BLOCK), jnp.float32),
                   jnp.zeros((N_MP * NG, BLOCK, BLOCK), jnp.float32),
                   jnp.zeros((D_WIN, FF_WIN), jnp.float32))
    final, unused = lax.scan(accumulate, start_state, (acts_split, grads_split))
    cov_a = final[0]
    cov_g = final[1]
    grad_sum = final[2]
    owners = jnp.arange(N_DP, dtype=jnp.int32)
    onehot = (owner_map[:, :, None] == owners[None, None, :]).astype(jnp.float32)
    a_strips = cov_a.reshape(NA, N_DP, STRIP, BLOCK)
    a_owned = jnp.einsum('ksd,ksrc->dkrc', onehot[:NA], a_strips, precision=lax.Precision.HIGHEST)
    g_strips = cov_g.reshape(N_MP, NG, N_DP, STRIP, BLOCK)
    g_owned = jnp.einsum('jsd,mjsrc->mdjrc', onehot[NA:], g_strips, precision=lax.Precision.HIGHEST)
    a_factor = decay_rate * old_a + (1.0 - decay_rate) * a_owned
    g_factor = decay_rate * old_g + (1.0 - decay_rate) * g_owned
    grad_low = grad_sum.astype(jnp.bfloat16).astype(jnp.float32)
    g_blocks = g_inverse.reshape(N_MP * NG, BLOCK, BLOCK).astype(jnp.float32)
    right_done = jnp.einsum('rjb,jbc->rjc', grad_low.reshape(D_WIN, N_MP * NG, BLOCK), g_blocks)
    right_done = right_done.astype(jnp.bfloat16).astype(jnp.float32).reshape(NA, BLOCK, FF_WIN)
    a_blocks = a_inverse.reshape(NA, BLOCK, BLOCK).astype(jnp.float32)
    result = jnp.einsum('kbc,kcf->kbf', a_blocks, right_done).astype(jnp.bfloat16)
    return a_factor, g_factor, result.reshape(D_WIN, N_MP, FF_DEV)
```

```python
import functools

import jax
import jax.numpy as jnp
from jax import lax
from jax.experimental import pallas as pl
from jax.experimental.pallas import tpu as pltpu
from jax.sharding import Mesh
from jax.sharding import PartitionSpec as P


BF = jnp.bfloat16
F32 = jnp.float32
BLOCK = 1024
TOK = 512
N_Y = 4
DECAY = 0.75
SUM_SCALE = 1.0 / 8192.0
VMEM_LIMIT = 50 * 1024 * 1024


def vmem():
    return pl.BlockSpec(memory_space=pltpu.VMEM)


def smem():
    return pl.BlockSpec(memory_space=pltpu.SMEM)


def shift(array, axis, by):
    count = lax.axis_size(axis)
    return lax.ppermute(array, axis, [(i, (i + by) % count) for i in range(count)])


def dot(a, b):
    return jnp.dot(a, b, preferred_element_type=F32)


def q_kernel(where, grads, ginv, own, other):
    zl, x, c = where[0], where[1], where[2]
    j = pl.program_id(0)
    q = dot(grads[...], ginv[...])
    for xd in range(4):
        first = q[:, xd * 256 : xd * 256 + 128]
        second = q[:, xd * 256 + 128 : xd * 256 + 256]
        mine = jnp.where(c == 0, first, second)
        theirs = jnp.where(c == 0, second, first)
        slot = ((xd - x) & 3) * 2 + (j ^ zl)
        own[slot] = mine.T.astype(BF)
        other[slot] = theirs.T.astype(BF)


def make_q(where, grads, ginv):
    shape = jax.ShapeDtypeStruct((8, 128, TOK), BF)
    whole = pl.BlockSpec((8, 128, TOK), lambda j: (0, 0, 0))
    return pl.pallas_call(
        q_kernel,
        grid=(2,),
        in_specs=[
            smem(),
            pl.BlockSpec((TOK, BLOCK), lambda j: (0, j)),
            pl.BlockSpec((BLOCK, BLOCK), lambda j: (j, 0)),
        ],
        out_specs=[whole, whole],
        out_shape=[shape, shape],
        compiler_params=pltpu.CompilerParams(vmem_limit_bytes=VMEM_LIMIT),
        cost_estimate=pl.CostEstimate(
            flops=2 * TOK * BLOCK * 2 * BLOCK, bytes_accessed=8 << 20, transcendentals=0
        ),
        name="make_q",
    )(where, grads, ginv)


def r_kernel(layout, q_own, q_other, acts_own, acts_other, *outs):
    left = q_own[...].reshape(8 * 128, TOK)
    right = q_other[...].reshape(8 * 128, TOK)
    part = dot(left, acts_own[...]) + dot(right, acts_other[...])
    for out, slots in zip(outs, layout):
        for at, slot in enumerate(slots):
            out[at] = part[slot * 128 : slot * 128 + 128].astype(BF)


def make_r(block, layout, q_own, q_other, acts_own, acts_other):
    tile = 256
    steps = BLOCK // tile
    whole = pl.BlockSpec((8, 128, TOK), lambda n: (0, 0, 0))
    rows = pl.BlockSpec((TOK, tile), lambda n: (0, block * steps + n))
    return pl.pallas_call(
        functools.partial(r_kernel, layout),
        grid=(steps,),
        in_specs=[whole, whole, rows, rows],
        out_specs=[pl.BlockSpec((len(s), 128, tile), lambda n: (0, 0, n)) for s in layout],
        out_shape=[jax.ShapeDtypeStruct((len(s), 128, BLOCK), BF) for s in layout],
        compiler_params=pltpu.CompilerParams(vmem_limit_bytes=VMEM_LIMIT),
        cost_estimate=pl.CostEstimate(
            flops=2 * BLOCK * BLOCK * BLOCK, bytes_accessed=6 << 20, transcendentals=0
        ),
        name=f"make_r{block}",
    )(q_own, q_other, acts_own, acts_other)


Z_FIRST = ((1, 3, 5, 7), (0, 2, 4, 6))
X_FIRST = ((4,), (5,), (2, 3), (6, 7), (0, 1))


def f_kernel(
    where, owner_map, g_own, g_other, a_own, a_other, p1, m1, k1, k3, k0, turned, pay
):
    zl, x, c, zh, y = where[0], where[1], where[2], where[3], where[4]
    m = zh * N_Y + y

    def slot_of(owner):
        return (((owner >> 1) & 3) - x & 3) * 2 + ((owner >> 3) ^ zl)

    turned[:, :TOK] = g_own[...].T
    turned[:, TOK:] = g_other[...].T
    for n in range(4):
        cols = slice(n * 256, n * 256 + 256)
        cov = dot(turned[:, :TOK], g_own[:, cols]) + dot(turned[:, TOK:], g_other[:, cols])
        cov = cov.astype(BF)
        for s in range(16):
            owner = owner_map[3 + c, s]
            slot, part = slot_of(owner), (owner & 1) * 8
            rows = cov[s * 64 : s * 64 + 64]
            pay[slot, part + 2 * n] = rows[:, :128]
            pay[slot, part + 2 * n + 1] = rows[:, 128:]
    for k in range(3):
        cols = pl.ds(pl.multiple_of(k * BLOCK + m * 128, 128), 128)
        rows = slice(k * BLOCK, k * BLOCK + BLOCK)
        cov = dot(a_own[:, cols].T, a_own[:, rows]) + dot(a_other[:, cols].T, a_other[:, rows])
        cov = cov.T.astype(BF)
        for s in range(16):
            owner = owner_map[k, s]
            slot = jnp.where((owner & 1) == c, slot_of(owner), 8)
            pay[slot, 16 + k] = cov[s * 64 : s * 64 + 64]
    p1[...] = pay[4]
    m1[...] = pay[5]
    k1[...] = pay[2:4]
    k3[...] = pay[6:8]
    k0[...] = pay[0:2]


def make_f(where, owner_map, g_own, g_other, a_own, a_other):
    one = jax.ShapeDtypeStruct((19, 64, 128), BF)
    two = jax.ShapeDtypeStruct((2, 19, 64, 128), BF)
    return pl.pallas_call(
        f_kernel,
        in_specs=[smem(), smem()] + [vmem()] * 4,
        out_specs=[vmem()] * 5,
        out_shape=[one, one, two, two, two],
        scratch_shapes=[
            pltpu.VMEM((BLOCK, 2 * TOK), BF),
            pltpu.VMEM((9, 19, 64, 128), BF),
        ],
        compiler_params=pltpu.CompilerParams(vmem_limit_bytes=VMEM_LIMIT),
        cost_estimate=pl.CostEstimate(
            flops=3 * BLOCK * BLOCK * BLOCK, bytes_accessed=12 << 20, transcendentals=0
        ),
        name="make_f",
    )(where, owner_map, g_own, g_other, a_own, a_other)


def wide(a, b):
    return a.astype(F32) + b.astype(F32)


def x_stage(p1, m1, k1, k3, k0):
    got_p = shift(p1, "x", 1)
    got_m = shift(m1, "x", -1)
    send_p = jnp.stack([wide(k1[0], got_p).astype(BF), k1[1]])
    send_m = jnp.stack([k3[0], wide(k3[1], got_m).astype(BF)])
    near_p = shift(send_p, "x", 1)
    near_m = shift(send_m, "x", -1)
    return wide(k0, near_p) + near_m.astype(F32)


def z_first(send, keep):
    total = wide(keep, shift(send, "zl", 1)).astype(BF)
    total = total.reshape(4, 2, 64, BLOCK)
    done = x_stage(total[2, 0], total[2, 1], total[1], total[3], total[0])
    return done.astype(BF).reshape(128, BLOCK)


def x_first(p1, m1, k1, k3, k0):
    total = x_stage(p1, m1, k1, k3, k0)
    return total[0] + shift(total[1].astype(BF), "zl", 1).astype(F32)


def assemble_kernel(where, *refs):
    zl, x, c, y = where[0], where[1], where[2], where[4]
    ins, out = refs[:-1], refs[-1]
    for at, ref in enumerate(ins):
        cb, dy = divmod(at, 4)
        col = pl.multiple_of(((y + dy) & 3) * 256, 256)

        @pl.loop(0, 8)
        def piece(i):
            dx, dz = i >> 1, i & 1
            d = ((zl ^ dz) * 4 + ((x + dx) & 3)) * 2 + (c ^ cb)
            row = pl.multiple_of(d * 192, 64)
            out[pl.ds(row, 192), pl.ds(col, 256)] = ref[dx, dz]


def gather_inverse(where, a_inverse):
    y = lax.axis_index("y")
    mine = lax.dynamic_slice_in_dim(a_inverse, y * 256, 256, axis=1)
    pair = jnp.stack([mine, shift(mine, "zl", 1)])
    quad = jnp.stack([pair, shift(pair, "x", -1), shift(pair, "x", 2), shift(pair, "x", 1)])
    rows = [quad, shift(quad, "y", -1), shift(quad, "y", 2), shift(quad, "y", 1)]
    rows += [shift(r, "c", 1) for r in rows]
    return pl.pallas_call(
        assemble_kernel,
        in_specs=[smem()] + [vmem()] * 8,
        out_specs=vmem(),
        out_shape=jax.ShapeDtypeStruct((3 * BLOCK, BLOCK), BF),
        compiler_params=pltpu.CompilerParams(vmem_limit_bytes=VMEM_LIMIT),
        cost_estimate=pl.CostEstimate(flops=0, bytes_accessed=12 << 20, transcendentals=0),
        name="assemble",
    )(where, *rows)


def g_end_kernel(where, own, got, old, out):
    c = where[2]
    for j in range(2):
        for n in range(8):
            cols = slice(n * 128, n * 128 + 128)
            new = jnp.where(j == c, own[c, n], got[n].astype(F32))
            out[0, 0, j, :, cols] = DECAY * old[0, 0, j, :, cols] + (1.0 - DECAY) * new


def a_end_kernel(where, r0, r1, r2, r3, old, out):
    zh, y = where[3], where[4]
    for dy, ref in enumerate((r0, r1, r2, r3)):
        for dz in range(2):
            col = pl.multiple_of(((zh ^ dz) * N_Y + ((y + dy) & 3)) * 128, 128)
            cols = pl.ds(col, 128)
            for k in range(3):
                new = ref[dz, k].astype(F32)
                out[0, k, :, cols] = DECAY * old[0, k, :, cols] + (1.0 - DECAY) * new


def finish_factors(where, total, old_a, old_g):
    c = lax.axis_index("c")
    g_part = total[:16].reshape(2, 8, 64, 128)
    theirs = lax.dynamic_index_in_dim(g_part, 1 - c, axis=0, keepdims=False).astype(BF)
    got = shift(theirs, "c", 1)
    g_factor = pl.pallas_call(
        g_end_kernel,
        in_specs=[smem()] + [vmem()] * 3,
        out_specs=vmem(),
        out_shape=jax.ShapeDtypeStruct(old_g.shape, F32),
        name="g_end",
    )(where, g_part, got, old_g)
    mine = (total[16:] * SUM_SCALE).astype(BF)
    pair = jnp.stack([mine, shift(mine, "zh", 1)])
    rows = [pair, shift(pair, "y", -1), shift(pair, "y", 2), shift(pair, "y", 1)]
    a_factor = pl.pallas_call(
        a_end_kernel,
        in_specs=[smem()] + [vmem()] * 5,
        out_specs=vmem(),
        out_shape=jax.ShapeDtypeStruct(old_a.shape, F32),
        name="a_end",
    )(where, *rows, old_a)
    return a_factor, g_factor


def per_device(acts, grads_out, old_a, old_g, a_inverse, g_inverse, owner_map):
    c = lax.axis_index("c")
    where = jnp.stack([lax.axis_index(n) for n in ("zl", "x", "c", "zh", "y")]).astype(jnp.int32)
    acts_other = shift(acts, "c", 1)
    theirs = lax.dynamic_slice_in_dim(grads_out, (1 - c) * BLOCK, BLOCK, axis=1)
    g_own = lax.dynamic_slice_in_dim(grads_out, c * BLOCK, BLOCK, axis=1)
    g_other = shift(theirs, "c", 1)
    q_own, q_theirs = make_q(where, grads_out, g_inverse)
    q_other = shift(q_theirs, "c", 1)
    inverse = gather_inverse(where, a_inverse)
    parts = make_f(where, owner_map, g_own, g_other, acts, acts_other)
    r0 = make_r(0, Z_FIRST, q_own, q_other, acts, acts_other)
    r2 = make_r(2, X_FIRST, q_own, q_other, acts, acts_other)
    r1 = make_r(1, Z_FIRST, q_own, q_other, acts, acts_other)
    factors = x_first(*parts)
    right = [z_first(*r0), z_first(*r1), x_first(r2[0][0], r2[1][0], *r2[2:]).astype(BF).reshape(128, BLOCK)]
    a_factor, g_factor = finish_factors(where, factors, old_a, old_g)
    result = [
        lax.dot_general(
            inverse[k * BLOCK : (k + 1) * BLOCK],
            right[k],
            (((1,), (1,)), ((), ())),
            preferred_element_type=F32,
        ).astype(BF)
        for k in range(3)
    ]
    return a_factor, g_factor, jnp.concatenate(result).reshape(3 * BLOCK, 1, 128)


def solution(mesh):
    fine = Mesh(mesh.devices.reshape(2, 4, 2, 2, 4), ("zl", "x", "c", "zh", "y"))
    dp, mp = ("zl", "x", "c"), ("zh", "y")
    return jax.shard_map(
        per_device,
        mesh=fine,
        in_specs=(
            P(dp, None),
            P(dp, mp),
            P(dp, None, None, None),
            P(mp, dp, None, None, None),
            P(dp, None),
            P(mp, None),
            P(),
        ),
        out_specs=(P(dp, None, None, None), P(mp, dp, None, None, None), P(None, mp, dp)),
        check_vma=False,
    )
```
